32 devices in a mesh: mem: 4 (over y, x), tile: 4 (over z), grp: 2 (over core).
Axes of the slice: x: 2, y: 2, z: 4, core: 2. Of those that a mesh axis runs over, the one named last changes fastest.
Arguments:
- members: float32 [3, 128, 64, 512], P(None, 'mem', ('tile', 'grp')), may hold values from -0.6 to 0.6
- obs_cells: int32 [8, 4, 1024], P(('tile', 'grp'), 'mem'), may hold values from 0 to 1023
- obs_count: int32 [8, 4], P(('tile', 'grp'), 'mem'), may hold values from 128 to 1024, as said below
- obs_values: float32 [8, 4, 1024], P(('tile', 'grp'), 'mem'), may hold values from -0.6 to 0.6
- obs_error: float32 [8, 4, 1024], P(('tile', 'grp'), 'mem'), may hold values from 0.03 to 0.3
- obs_noise: float32 [8, 4, 1024, 128], P(('tile', 'grp'), 'mem'), may hold values from -6 to 6
Outputs:
- analysis: bfloat16 [3, 128, 64, 512], P(None, None, ('tile', 'grp'), 'mem')
The draws below stay inside these ranges and needn't reach their ends.
Inputs may be any that keep to these rules, and one draw needn't show every extreme that they name: `obs_count`: a multiple of 128; some tile has exactly 1024 live slots in every draw.
All inputs are finite; a program needn't handle non-finite values.
Results may differ from the reference program's by a relative error of at most 0.0058.
Values may be sent and summed in bfloat16 or wider, within the bound.
A program may use at most 64 MiB of HBM per device.

```python
import math
import jax
import jax.numpy as jnp
from jax import lax

STRIP_LINES = 8
DOMAIN_VERTICALS = 512
STEPS = 4
OBS_CAP = 1024
REALIZATION_NUM = 128
DOMAIN_LINES = 64
PATCHES_SOUTHWARD = 8
PATCHES_EASTWARD = 4
PATCH_BREADTH = 128
PATCH_POINTS = 1024


def draw_obs_count(key, part):
    key_one, key_two, key_three = jax.random.split(jax.random.fold_in(key, 17), 3)
    blocks_most = OBS_CAP // 128
    factor_one = jax.random.randint(key_one, (PATCHES_SOUTHWARD, PATCHES_EASTWARD), 0, blocks_most)
    factor_two = jax.random.randint(key_two, (PATCHES_SOUTHWARD, PATCHES_EASTWARD), 0, blocks_most)
    block_count = 1 + factor_one * factor_two // (blocks_most - 1)
    position = jax.random.randint(key_three, (), 0, PATCHES_SOUTHWARD * PATCHES_EASTWARD)
    flattened = block_count.reshape(-1).at[position].set(blocks_most)
    return (flattened * 128).reshape(PATCHES_SOUTHWARD, PATCHES_EASTWARD).astype(jnp.int32)


def touch_ends(entries, key, smallest, largest):
    longest = entries.shape.index(max(entries.shape))
    spots = []
    for shift in (0, 1):
        where = [jax.random.randint(jax.random.fold_in(key, axis), (), 0, length) for axis, length in enumerate(entries.shape)]
        where[longest] = (where[longest] + shift) % entries.shape[longest]
        spots.append(tuple(where))
    return entries.at[spots[0]].set(smallest).at[spots[1]].set(largest)


def steps_of(own_key, dims, pieces, smallest, largest):
    def one(dim, parts):
        steps = jax.random.uniform(jax.random.fold_in(jax.random.fold_in(own_key, 6), dim), (parts,), jnp.float32, smallest / len(pieces), largest / len(pieces))
        return jnp.repeat(jnp.exp(steps), dims[dim] // parts).reshape((-1,) + (1,) * (len(dims) - dim - 1))

    gain = one(*pieces[0])
    for cut in pieces[1:]:
        gain = gain * one(*cut)
    return gain


def centred(key, extent, width, most, cuts=(), held_as=jnp.bfloat16):
    factor_of = steps_of(key, extent, cuts, -0.22, 0.18) if cuts else 1.0
    values = jax.random.normal(key, extent, jnp.float32) * width * factor_of
    return jnp.minimum(jnp.maximum(values, -most), most).astype(held_as)


def setup_inputs(seed: int = 0) -> dict:
    seeds = jax.random.split(jax.random.key(seed), 7)
    members = centred(seeds[0], (3, REALIZATION_NUM, DOMAIN_LINES, DOMAIN_VERTICALS), 0.1, 0.6, ((1, 4), (2, 8)), jnp.float32)
    obs_cells = touch_ends(jax.random.randint(seeds[1], (PATCHES_SOUTHWARD, PATCHES_EASTWARD, OBS_CAP), 0, PATCH_POINTS), jax.random.fold_in(seeds[1], 1), 0, PATCH_POINTS - 1).astype(jnp.int32)
    obs_count = draw_obs_count(jax.random.fold_in(seeds[6], 71), 0)
    obs_values = centred(seeds[3], (PATCHES_SOUTHWARD, PATCHES_EASTWARD, OBS_CAP), 0.1, 0.6, ((0, 8), (1, 4)), jnp.float32)
    obs_error = jnp.clip(jnp.exp(math.log(0.3) - 2.3025852 * jax.random.uniform(seeds[4], (PATCHES_SOUTHWARD, PATCHES_EASTWARD, OBS_CAP), jnp.float32) ** steps_of(seeds[4], (PATCHES_SOUTHWARD, PATCHES_EASTWARD, OBS_CAP), ((0, 8), (1, 4)), -0.2, 0.2)), 0.03, 0.3)
    obs_noise = centred(seeds[5], (PATCHES_SOUTHWARD, PATCHES_EASTWARD, OBS_CAP, REALIZATION_NUM), 1.0, 6.0, ((0, 8), (1, 4)), jnp.float32)
    return dict(members=members, obs_cells=obs_cells, obs_count=obs_count, obs_values=obs_values, obs_error=obs_error, obs_noise=obs_noise)


courant = 0.3
gravity = 1.0
coriolis = 0.1

def beside_all(field_e, field_w, field_n, field_s):
    return 0.25 * (field_e + field_w + field_n + field_s)

def advance(padded):
    height = padded[0]
    zonal = padded[1]
    meridional = padded[2]
    height_e, height_w, height_mid = (height[:, 2:, :], height[:, :-2, :], height[:, 1:-1, :])
    zonal_e, zonal_w, zonal_mid = (zonal[:, 2:, :], zonal[:, :-2, :], zonal[:, 1:-1, :])
    merid_e, merid_w, merid_mid = (meridional[:, 2:, :], meridional[:, :-2, :], meridional[:, 1:-1, :])
    height_n, height_s = (jnp.roll(height_mid, -1, axis=2), jnp.roll(height_mid, 1, axis=2))
    zonal_n, zonal_s = (jnp.roll(zonal_mid, -1, axis=2), jnp.roll(zonal_mid, 1, axis=2))
    merid_n, merid_s = (jnp.roll(merid_mid, -1, axis=2), jnp.roll(merid_mid, 1, axis=2))
    new_height = beside_all(height_e, height_w, height_n, height_s) - courant * ((1.0 + height_e) * zonal_e - (1.0 + height_w) * zonal_w) - courant * ((1.0 + height_n) * merid_n - (1.0 + height_s) * merid_s)
    new_zonal = beside_all(zonal_e, zonal_w, zonal_n, zonal_s) - courant * (0.5 * zonal_e * zonal_e + gravity * height_e - (0.5 * zonal_w * zonal_w + gravity * height_w)) - courant * merid_mid * (zonal_n - zonal_s) + coriolis * merid_mid
    new_merid = beside_all(merid_e, merid_w, merid_n, merid_s) - courant * (0.5 * merid_n * merid_n + gravity * height_n - (0.5 * merid_s * merid_s + gravity * height_s)) - courant * zonal_mid * (merid_e - merid_w) - coriolis * zonal_mid
    return jnp.stack([new_height, new_zonal, new_merid])

def predict_realization_group(fluid_condition):
    for step_index in range(STEPS):
        padded = jnp.concatenate([fluid_condition[:, :, -1:, :], fluid_condition, fluid_condition[:, :, :1, :]], axis=2)
        fluid_condition = advance(padded)
    return fluid_condition

def analyse(fields, cell_ids, live_count, obs_vals, obs_std, perturb):
    ens_size = fields.shape[1]
    states = fields.astype(jnp.float32)
    spread = states - jnp.mean(states, axis=1, keepdims=True)
    observed = jnp.take(states[0], cell_ids, axis=1)
    obs_spread = observed - jnp.mean(observed, axis=0, keepdims=True)
    slot_ids = jnp.arange(obs_vals.shape[0], dtype=jnp.int32)
    weights = jnp.where(slot_ids < live_count, 1.0 / (obs_std * obs_std), 0.0).astype(jnp.float32)
    weighted = obs_spread * weights[None, :]
    innov = obs_vals[None, :] + obs_std[None, :] * perturb.T - observed
    gram = (ens_size - 1.0) * jnp.eye(ens_size, dtype=jnp.float32) + jnp.dot(weighted, obs_spread.T, precision=lax.Precision.HIGHEST)
    rhs_matrix = jnp.dot(weighted, innov.T, precision=lax.Precision.HIGHEST)
    factor = jnp.linalg.cholesky(gram)
    weight_matrix = jax.scipy.linalg.cho_solve((factor, True), rhs_matrix)
    update = jnp.einsum('vkc,kj->vjc', spread, weight_matrix, precision=lax.Precision.HIGHEST)
    return (states + update).astype(jnp.bfloat16)

def reference(members, obs_cells, obs_count, obs_values, obs_error, obs_noise):
    batch_size = math.gcd(REALIZATION_NUM, 16)
    realization_groups = jnp.moveaxis(members.reshape(3, REALIZATION_NUM // batch_size, batch_size, DOMAIN_LINES, DOMAIN_VERTICALS), 1, 0)
    advanced_conditions = lax.map(predict_realization_group, realization_groups)
    predict_realizations = jnp.moveaxis(advanced_conditions, 0, 1).reshape(3, REALIZATION_NUM, DOMAIN_LINES, DOMAIN_VERTICALS).astype(jnp.bfloat16)
    condition_patches = predict_realizations.reshape(3, REALIZATION_NUM, PATCHES_SOUTHWARD, STRIP_LINES, PATCHES_EASTWARD, PATCH_BREADTH).transpose(2, 4, 0, 1, 3, 5).reshape(PATCHES_SOUTHWARD * PATCHES_EASTWARD, 3, REALIZATION_NUM, PATCH_POINTS)
    results = lax.map(lambda item: analyse(*item), (condition_patches, obs_cells.reshape(PATCHES_SOUTHWARD * PATCHES_EASTWARD, OBS_CAP), obs_count.reshape(PATCHES_SOUTHWARD * PATCHES_EASTWARD), obs_values.reshape(PATCHES_SOUTHWARD * PATCHES_EASTWARD, OBS_CAP), obs_error.reshape(PATCHES_SOUTHWARD * PATCHES_EASTWARD, OBS_CAP), obs_noise.reshape(PATCHES_SOUTHWARD * PATCHES_EASTWARD, OBS_CAP, REALIZATION_NUM)))
    return results.reshape(PATCHES_SOUTHWARD, PATCHES_EASTWARD, 3, REALIZATION_NUM, STRIP_LINES, PATCH_BREADTH).transpose(2, 3, 0, 4, 1, 5).reshape(3, REALIZATION_NUM, DOMAIN_LINES, DOMAIN_VERTICALS)
```

```python
import functools

import jax
import jax.numpy as jnp
from jax import lax
from jax.experimental import pallas as pl
from jax.experimental.pallas import tpu as pltpu
from jax.sharding import PartitionSpec as P

STEPS = 4

courant = 0.3
gravity = 1.0
coriolis = 0.1
HIGHEST = lax.Precision.HIGHEST
VMEM_BYTES = 50 * 1024 * 1024


def advance(west, mid, east):
    (hw, uw, vw), (h, u, v), (he, ue, ve) = west, mid, east
    cols = h.shape[1]
    north = lambda q: pltpu.roll(q, cols - 1, 1)
    south = lambda q: pltpu.roll(q, 1, 1)
    hn, hs, un, us, vn, vs = north(h), south(h), north(u), south(u), north(v), south(v)
    new_h = (
        0.25 * (he + hw + hn + hs)
        - courant * ((1.0 + he) * ue - (1.0 + hw) * uw)
        - courant * ((1.0 + hn) * vn - (1.0 + hs) * vs)
    )
    new_u = (
        0.25 * (ue + uw + un + us)
        - courant * ((0.5 * ue * ue + gravity * he) - (0.5 * uw * uw + gravity * hw))
        - courant * v * (un - us)
        + coriolis * v
    )
    new_v = (
        0.25 * (ve + vw + vn + vs)
        - courant * ((0.5 * vn * vn + gravity * hn) - (0.5 * vs * vs + gravity * hs))
        - courant * u * (ve - vw)
        - coriolis * u
    )
    return new_h, new_u, new_v


def forecast_kernel(members, low, high, out, first, second):
    fields, ens, rows, cols = members.shape
    width = low.shape[1]
    parts, tile_cols = out.shape[0], out.shape[4]
    for f in range(fields):
        for r in range(width):
            first[r, f] = low[f, r].astype(jnp.float32)
            first[width + rows + r, f] = high[f, r].astype(jnp.float32)
        for r in range(rows):
            first[width + r, f] = members[f, :, r, :]
    buffers = (first, second)
    for step in range(STEPS):
        src, dst = buffers[step % 2], buffers[(step + 1) % 2]
        start = step + 1
        count = rows + 2 * width - 2 * start
        last = step == STEPS - 1

        def row_step(i, carry, src=src, dst=dst, start=start, last=last):
            row = i + start

            def at(which, m):
                return [src[which, f, pl.ds(m, 8), :] for f in range(fields)]

            for m in range(0, ens, 16):
                done = []
                for half in (m, m + 8):
                    done.append(advance(at(row - 1, half), at(row, half), at(row + 1, half)))
                    if not last:
                        for f in range(fields):
                            dst[row, f, pl.ds(half, 8), :] = done[-1][f]
                if last:
                    for f in range(fields):
                        both = jnp.concatenate([done[0][f], done[1][f]], axis=0)
                        both = both.astype(jnp.bfloat16)
                        for d in range(parts):
                            out[d, f, i, pl.ds(m, 16), :] = both[:, d * tile_cols : (d + 1) * tile_cols]
            return carry

        lax.fori_loop(0, count, row_step, 0)


def eliminate(gram, rhs):
    size = gram.shape[0]
    group = lax.broadcasted_iota(jnp.int32, (8, size), 0)

    def block(_, carry):
        a, b = carry
        for j in range(8):
            row_a, row_b = a[j : j + 1, :], b[j : j + 1, :]
            col = a[:, j : j + 1]
            inverse = 1.0 / a[j : j + 1, j : j + 1]
            row_a, row_b = row_a * inverse, row_b * inverse
            new_a, new_b = a - col * row_a, b - col * row_b
            a = jnp.concatenate([jnp.where(group == j, row_a, new_a[:8]), new_a[8:]], axis=0)
            b = jnp.concatenate([jnp.where(group == j, row_b, new_b[:8]), new_b[8:]], axis=0)
        a = pltpu.roll(jnp.concatenate([a[8:], a[:8]], axis=0), size - 8, 1)
        b = jnp.concatenate([b[8:], b[:8]], axis=0)
        return a, b

    return lax.fori_loop(0, size // 8, block, (gram, rhs))[1]


def analysis_kernel(recv, count, cells, values, error, noise, out, state, tall):
    parts, fields, rows, part_ens, cols = recv.shape
    ens = parts * part_ens
    points = rows * cols
    for s in range(parts):
        for f in range(fields):
            for r in range(rows):
                state[f, s * part_ens : (s + 1) * part_ens, r * cols : (r + 1) * cols] = recv[s, f, r]
    slots = cells.shape[1]
    observed = jnp.zeros((ens, slots), jnp.float32)
    chunk = 256 if points % 256 == 0 else cols
    for c in range(0, points, chunk):
        ids = lax.broadcasted_iota(jnp.int32, (chunk, slots), 0) + c
        pick = jnp.where(ids == cells[...], 1.0, 0.0).astype(jnp.bfloat16)
        observed += jnp.dot(state[0, :, c : c + chunk], pick, preferred_element_type=jnp.float32)
    mean = jnp.sum(observed, axis=0, keepdims=True) * (1.0 / ens)
    spread = observed - mean
    std = error[...]
    slot_ids = lax.broadcasted_iota(jnp.int32, (1, slots), 1)
    weights = jnp.where(slot_ids < count[0, 0], 1.0 / (std * std), 0.0)
    weighted = spread * weights
    gram0 = lax.dot_general(
        weighted, spread, (((1,), (1,)), ((), ())), precision=HIGHEST, preferred_element_type=jnp.float32
    )
    rhs = jnp.dot(weighted * std, noise[...], precision=HIGHEST, preferred_element_type=jnp.float32)
    rhs = rhs + jnp.sum(weighted * (values[...] - mean), axis=1, keepdims=True) - gram0
    eye = jnp.where(
        lax.broadcasted_iota(jnp.int32, (ens, ens), 0) == lax.broadcasted_iota(jnp.int32, (ens, ens), 1), 1.0, 0.0
    )
    solved = eliminate(gram0 + (ens - 1.0) * eye, rhs)
    centred = solved - jnp.sum(solved, axis=0, keepdims=True) * (1.0 / ens) + eye
    turned = centred.T
    upper = turned.astype(jnp.bfloat16)
    lower = (turned - upper.astype(jnp.float32)).astype(jnp.bfloat16)
    for f in range(fields):
        for r in range(rows):
            block = state[f, :, r * cols : (r + 1) * cols]
            tall[:, r, :] = jnp.dot(upper, block, preferred_element_type=jnp.float32) + jnp.dot(
                lower, block, preferred_element_type=jnp.float32
            )
        out[f] = tall[...].astype(jnp.bfloat16)


def vmem():
    return pl.BlockSpec(memory_space=pltpu.VMEM)


def body(members, obs_cells, obs_count, obs_values, obs_error, obs_noise):
    axes = ("tile", "grp")
    count = lax.axis_size(axes)
    forward = [(i, (i + 1) % count) for i in range(count)]
    backward = [(t, s) for s, t in forward]
    fields, ens, rows, cols = members.shape
    parts = lax.axis_size("mem")
    edge = lambda x: jnp.swapaxes(x, 1, 2).astype(jnp.bfloat16)
    low = lax.ppermute(edge(members[:, :, rows - STEPS :, :]), axes, forward)
    high = lax.ppermute(edge(members[:, :, :STEPS, :]), axes, backward)
    tile_cols = cols // parts
    ready = pl.pallas_call(
        forecast_kernel,
        name="forecast",
        out_shape=jax.ShapeDtypeStruct((parts, fields, rows, ens, tile_cols), jnp.bfloat16),
        in_specs=[vmem()] * 3,
        out_specs=vmem(),
        scratch_shapes=[pltpu.VMEM((rows + 2 * STEPS, fields, ens, cols), jnp.float32)] * 2,
        compiler_params=pltpu.CompilerParams(vmem_limit_bytes=VMEM_BYTES),
    )(members, low, high)
    recv = lax.all_to_all(ready, "mem", split_axis=0, concat_axis=0)
    full = ens * parts
    return pl.pallas_call(
        analysis_kernel,
        name="analysis",
        out_shape=jax.ShapeDtypeStruct((fields, full, rows, tile_cols), jnp.bfloat16),
        in_specs=[vmem(), pl.BlockSpec(memory_space=pltpu.SMEM)] + [vmem()] * 4,
        out_specs=vmem(),
        scratch_shapes=[
            pltpu.VMEM((fields, full, rows * tile_cols), jnp.bfloat16),
            pltpu.VMEM((full, rows, tile_cols), jnp.float32),
        ],
        compiler_params=pltpu.CompilerParams(vmem_limit_bytes=VMEM_BYTES),
    )(recv, obs_count, obs_cells[0], obs_values[0], obs_error[0], obs_noise[0, 0])


def solution(mesh):
    in_specs = (
        P(None, "mem", ("tile", "grp"), None),
        P(("tile", "grp"), "mem", None),
        P(("tile", "grp"), "mem"),
        P(("tile", "grp"), "mem", None),
        P(("tile", "grp"), "mem", None),
        P(("tile", "grp"), "mem", None, None),
    )
    out_specs = P(None, None, ("tile", "grp"), "mem")
    return jax.shard_map(body, mesh=mesh, in_specs=in_specs, out_specs=out_specs, check_vma=False)
```

```python
import jax
import jax.numpy as jnp
from jax import lax
from jax.experimental import pallas as pl
from jax.experimental.pallas import tpu as pltpu
from jax.sharding import PartitionSpec as P

STEPS = 4

courant = 0.3
gravity = 1.0
coriolis = 0.1
HIGHEST = lax.Precision.HIGHEST
VMEM_BYTES = 50 * 1024 * 1024


def advance(west, mid, east):
    (hw, uw, vw), (h, u, v), (he, ue, ve) = west, mid, east
    cols = h.shape[1]
    north = lambda q: pltpu.roll(q, cols - 1, 1)
    south = lambda q: pltpu.roll(q, 1, 1)
    hn, hs, un, us, vn, vs = north(h), south(h), north(u), south(u), north(v), south(v)
    new_h = (
        0.25 * (he + hw + hn + hs)
        - courant * ((1.0 + he) * ue - (1.0 + hw) * uw)
        - courant * ((1.0 + hn) * vn - (1.0 + hs) * vs)
    )
    new_u = (
        0.25 * (ue + uw + un + us)
        - courant * ((0.5 * ue * ue + gravity * he) - (0.5 * uw * uw + gravity * hw))
        - courant * v * (un - us)
        + coriolis * v
    )
    new_v = (
        0.25 * (ve + vw + vn + vs)
        - courant * ((0.5 * vn * vn + gravity * hn) - (0.5 * vs * vs + gravity * hs))
        - courant * u * (ve - vw)
        - coriolis * u
    )
    return new_h, new_u, new_v


def eliminate(gram, rhs):
    size = gram.shape[0]
    group = lax.broadcasted_iota(jnp.int32, (8, size), 0)

    def block(_, carry):
        a, b = carry
        for j in range(8):
            row_a, row_b = a[j : j + 1, :], b[j : j + 1, :]
            col = a[:, j : j + 1]
            inverse = 1.0 / a[j : j + 1, j : j + 1]
            row_a, row_b = row_a * inverse, row_b * inverse
            new_a, new_b = a - col * row_a, b - col * row_b
            a = jnp.concatenate([jnp.where(group == j, row_a, new_a[:8]), new_a[8:]], axis=0)
            b = jnp.concatenate([jnp.where(group == j, row_b, new_b[:8]), new_b[8:]], axis=0)
        a = pltpu.roll(jnp.concatenate([a[8:], a[:8]], axis=0), size - 8, 1)
        b = jnp.concatenate([b[8:], b[:8]], axis=0)
        return a, b

    return lax.fori_loop(0, size // 8, block, (gram, rhs))[1]


def neighbour_ids():
    groups = lax.axis_size("grp")
    total = lax.axis_size("tile") * groups
    me = lax.axis_index("tile") * groups + lax.axis_index("grp")
    after, before = lax.rem(me + 1, total), lax.rem(me + total - 1, total)
    return [{"tile": i // groups, "grp": lax.rem(i, groups)} for i in (after, before)]


def kernel(
    members, count, cells, values, error, noise, out,
    first, second, edges, halo, ready, recv, state, pick, tall,
    halo_send, halo_recv, part_send, part_recv,
):
    fields, ens, rows, cols = members.shape
    width = STEPS
    parts, _, _, _, tile_cols = ready.shape
    full = parts * ens
    points = rows * tile_cols
    slots = cells.shape[1]
    me = lax.axis_index("mem")
    after, before = neighbour_ids()
    peers = [lax.rem(me + p, parts) for p in range(1, parts)]
    targets = [after, before] + [{"mem": p} for p in peers]

    barrier = pltpu.get_barrier_semaphore()
    for target in targets:
        pl.semaphore_signal(barrier, inc=1, device_id=target, device_id_type=pl.DeviceIdType.MESH)
    for f in range(fields):
        for r in range(rows):
            row = members[f, :, r, :]
            first[width + r, f] = row
            if r >= rows - width:
                edges[0, f, r - (rows - width)] = row.astype(jnp.bfloat16)
            if r < width:
                edges[1, f, r] = row.astype(jnp.bfloat16)
    pl.semaphore_wait(barrier, len(targets))

    halo_copies = []
    for way, target in enumerate((after, before)):
        copy = pltpu.make_async_remote_copy(
            src_ref=edges.at[way],
            dst_ref=halo.at[way],
            send_sem=halo_send.at[way],
            recv_sem=halo_recv.at[way],
            device_id=target,
            device_id_type=pl.DeviceIdType.MESH,
        )
        copy.start()
        halo_copies.append(copy)

    buffers = (first, second)

    def run_rows(step, start, number):
        src, dst = buffers[step % 2], buffers[(step + 1) % 2]
        last = step == STEPS - 1

        def row_step(i, carry):
            row = i + start

            def at(which, m):
                return [src[which, f, pl.ds(m, 8), :] for f in range(fields)]

            for m in range(0, ens, 16):
                done = []
                for half in (m, m + 8):
                    done.append(advance(at(row - 1, half), at(row, half), at(row + 1, half)))
                    if not last:
                        for f in range(fields):
                            dst[row, f, pl.ds(half, 8), :] = done[-1][f]
                if last:
                    for f in range(fields):
                        both = jnp.concatenate([done[0][f], done[1][f]], axis=0)
                        both = both.astype(jnp.bfloat16)
                        for d in range(parts):
                            ready[d, f, row - width, pl.ds(m, 16), :] = both[:, d * tile_cols : (d + 1) * tile_cols]
            return carry

        lax.fori_loop(0, number, row_step, 0)

    for step in range(STEPS):
        inner = rows - 2 * (step + 1)
        if inner > 0:
            run_rows(step, width + step + 1, inner)
    chunk = 256 if points % 256 == 0 else tile_cols

    def select(i, carry):
        ids = lax.broadcasted_iota(jnp.int32, (chunk, slots), 0) + i * chunk
        start = pl.multiple_of(i * chunk, chunk)
        pick[pl.ds(start, chunk), :] = jnp.where(ids == cells[...], 1.0, 0.0).astype(jnp.bfloat16)
        return carry

    lax.fori_loop(0, points // chunk, select, 0)

    for copy in halo_copies:
        copy.wait_recv()
    for f in range(fields):
        for r in range(width):
            first[r, f] = halo[0, f, r].astype(jnp.float32)
            first[width + rows + r, f] = halo[1, f, r].astype(jnp.float32)

    sent = []

    def send(piece, f, row, number):
        group = []
        for p, peer in enumerate(peers):
            copy = pltpu.make_async_remote_copy(
                src_ref=ready.at[peer, f, pl.ds(row, number)],
                dst_ref=recv.at[me, f, pl.ds(row, number)],
                send_sem=part_send.at[piece, p],
                recv_sem=part_recv.at[piece, p],
                device_id={"mem": peer},
                device_id_type=pl.DeviceIdType.MESH,
            )
            copy.start()
            group.append(copy)
        sent.append(group)

    for step in range(STEPS - 1):
        edge = step + 1
        low_end = max(width + step + 1, edge)
        high_start = width + rows - (step + 1)
        if high_start > low_end:
            run_rows(step, edge, low_end - edge)
            run_rows(step, high_start, rows + 2 * width - edge - high_start)
        else:
            run_rows(step, edge, rows + 2 * width - 2 * edge)
    half_rows = rows // 2
    run_rows(STEPS - 1, width, half_rows)
    send(0, 0, 0, half_rows)
    run_rows(STEPS - 1, width + half_rows, rows - half_rows)
    send(1, 0, half_rows, rows - half_rows)
    for f in range(1, fields):
        send(f + 1, f, 0, rows)

    def place(f):
        recv[me, f] = ready[me, f]
        for s in range(parts):
            for r in range(rows):
                state[f, s * ens : (s + 1) * ens, r * tile_cols : (r + 1) * tile_cols] = recv[s, f, r]

    for group in sent[:2]:
        for copy in group:
            copy.wait_recv()
    place(0)
    observed = jnp.dot(state[0], pick[...], preferred_element_type=jnp.float32)
    mean = jnp.sum(observed, axis=0, keepdims=True) * (1.0 / full)
    spread = observed - mean
    std = error[...]
    slot_ids = lax.broadcasted_iota(jnp.int32, (1, slots), 1)
    weights = jnp.where(slot_ids < count[0, 0], 1.0 / (std * std), 0.0)
    weighted = spread * weights
    gram0 = lax.dot_general(
        weighted, spread, (((1,), (1,)), ((), ())), precision=HIGHEST, preferred_element_type=jnp.float32
    )
    rhs = jnp.dot(weighted * std, noise[...], precision=HIGHEST, preferred_element_type=jnp.float32)
    rhs = rhs + jnp.sum(weighted * (values[...] - mean), axis=1, keepdims=True) - gram0
    eye = jnp.where(
        lax.broadcasted_iota(jnp.int32, (full, full), 0) == lax.broadcasted_iota(jnp.int32, (full, full), 1), 1.0, 0.0
    )
    solved = eliminate(gram0 + (full - 1.0) * eye, rhs)
    centred = solved - jnp.sum(solved, axis=0, keepdims=True) * (1.0 / full) + eye
    turned = centred.T
    upper = turned.astype(jnp.bfloat16)
    lower = (turned - upper.astype(jnp.float32)).astype(jnp.bfloat16)
    for f in range(fields):
        if f > 0:
            for copy in sent[f + 1]:
                copy.wait_recv()
            place(f)
        for r in range(rows):
            block = state[f, :, r * tile_cols : (r + 1) * tile_cols]
            tall[:, r, :] = jnp.dot(upper, block, preferred_element_type=jnp.float32) + jnp.dot(
                lower, block, preferred_element_type=jnp.float32
            )
        out[f] = tall[...].astype(jnp.bfloat16)
    for copy in halo_copies:
        copy.wait_send()
    for group in sent:
        for copy in group:
            copy.wait_send()


def vmem():
    return pl.BlockSpec(memory_space=pltpu.VMEM)


def body(members, obs_cells, obs_count, obs_values, obs_error, obs_noise):
    fields, ens, rows, cols = members.shape
    parts = lax.axis_size("mem")
    tile_cols = cols // parts
    full = ens * parts
    points = rows * tile_cols
    slots = obs_cells.shape[2]
    pieces = fields + 1
    shared = pltpu.VMEM((rows + 2 * STEPS, fields, ens, cols), jnp.float32)
    edge = pltpu.VMEM((2, fields, STEPS, ens, cols), jnp.bfloat16)
    part = pltpu.VMEM((parts, fields, rows, ens, tile_cols), jnp.bfloat16)
    return pl.pallas_call(
        kernel,
        name="assimilate",
        out_shape=jax.ShapeDtypeStruct((fields, full, rows, tile_cols), jnp.bfloat16),
        in_specs=[vmem(), pl.BlockSpec(memory_space=pltpu.SMEM)] + [vmem()] * 4,
        out_specs=vmem(),
        scratch_shapes=[
            shared,
            shared,
            edge,
            edge,
            part,
            part,
            pltpu.VMEM((fields, full, points), jnp.bfloat16),
            pltpu.VMEM((points, slots), jnp.bfloat16),
            pltpu.VMEM((full, rows, tile_cols), jnp.float32),
            pltpu.SemaphoreType.DMA((2,)),
            pltpu.SemaphoreType.DMA((2,)),
            pltpu.SemaphoreType.DMA((pieces, parts - 1)),
            pltpu.SemaphoreType.DMA((pieces, parts - 1)),
        ],
        compiler_params=pltpu.CompilerParams(
            vmem_limit_bytes=VMEM_BYTES, collective_id=0, has_side_effects=True
        ),
    )(members, obs_count, obs_cells[0], obs_values[0], obs_error[0], obs_noise[0, 0])


def solution(mesh):
    in_specs = (
        P(None, "mem", ("tile", "grp"), None),
        P(("tile", "grp"), "mem", None),
        P(("tile", "grp"), "mem"),
        P(("tile", "grp"), "mem", None),
        P(("tile", "grp"), "mem", None),
        P(("tile", "grp"), "mem", None, None),
    )
    out_specs = P(None, None, ("tile", "grp"), "mem")
    return jax.shard_map(body, mesh=mesh, in_specs=in_specs, out_specs=out_specs, check_vma=False)
```
